32 devices in a mesh: row: 2 (over x), col: 16 (over z, y, core).
Axes of the slice: x: 2, y: 2, z: 4, core: 2. Of those that a mesh axis runs over, the one named last changes fastest.
Arguments:
- projector: float32 [18432, 18432], P('row', 'col'), may hold values from -9 to 490, as said below
- saved: float32 [18432, 512], P('col', 'row'), may hold values from -0.0048828125 to 0.0048828125
- grad_slab: float32 [512, 18432], P('col', 'row'), may hold values from -0.03125 to 0.03125
Outputs:
- updated: float32 [18432, 18432], P('row', 'col')
- projected: float32 [512, 18432], P('row', 'col')
The draws below stay inside these ranges and needn't reach their ends.
Inputs may be any that keep to these rules, and one draw needn't show every extreme that they name: projector is symmetric and positive definite, every eigenvalue above 100; its diagonal entries lie between 390 and 490.
All inputs are finite; a program needn't handle non-finite values.
Results may differ from the reference program's by a relative error of at most 0.000071.
Values sent between devices are 32-bit elements; how exact they have to be, the bound alone decides.
No kernel may reach another device: no remote copies, remote signals or barrier semaphores. Data moves between devices by JAX's collectives and lax.ppermute only.
A program may use at most 192 MiB of HBM per device.

```python
import jax
import jax.numpy as jnp
from jax import lax

D = 18432
K = 512
R = 512


def draw_projector(key, part):
    base_key = jax.random.fold_in(key, 17)
    entry_key, diag_key = jax.random.split(base_key)
    raw = jax.random.truncated_normal(entry_key, -6.0, 6.0, (D, D), jnp.float32)
    symmetric = (raw + raw.T) * 0.70710678
    lifted = jax.random.uniform(diag_key, (D,), jnp.float32, 400.0, 480.0)
    index = jnp.arange(D)
    return symmetric.at[index, index].add(lifted)


def block_levels(key, shape, cuts, smallest, largest):
    factor_of = 1.0
    for position, parts in cuts:
        heights = jax.random.uniform(jax.random.fold_in(jax.random.fold_in(key, 6), position), (parts,), jnp.float32, smallest / len(cuts), largest / len(cuts))
        factor_of = factor_of * jnp.repeat(jnp.exp(heights), shape[position] // parts).reshape((-1,) + (1,) * (len(shape) - 1 - position))
    return factor_of


def normal_values(key, extent, scale, bound, shards=(), held_as=jnp.bfloat16):
    array = scale * jax.random.normal(key, extent, jnp.float32)
    if shards:
        array = array * block_levels(key, extent, shards, -0.22, 0.18)
    return jnp.clip(array, -bound, bound).astype(held_as)


def setup_inputs(seed: int = 0) -> dict:
    key_of = jax.random.split(jax.random.key(seed), 4)
    return {
        "projector": draw_projector(jax.random.fold_in(key_of[3], 71), 0),
        "saved": normal_values(key_of[1], (D, K), (1.0 / (21 * D ** 0.5)), 0.0048828125, ((0, 16), (1, 2)), jnp.float32),
        "grad_slab": normal_values(key_of[2], (R, D), 0.002, 0.03125, ((0, 16), (1, 2)), jnp.float32),
    }


def reference(projector, saved, grad_slab):
    highest = lax.Precision.HIGHEST
    y_all = jnp.dot(projector.astype(jnp.float32), saved.astype(jnp.float32), precision=highest, preferred_element_type=jnp.float32)
    system = jnp.eye(K, dtype=jnp.float32) + jnp.dot(saved.T.astype(jnp.float32), y_all.astype(jnp.float32), precision=highest, preferred_element_type=jnp.float32)
    factor = jnp.linalg.cholesky(system)
    solved = jax.scipy.linalg.cho_solve((factor, True), y_all.T)
    blocks = projector.reshape(8, D // 8, D)
    y_blocks = y_all.reshape(8, D // 8, K)
    g_blocks = grad_slab.reshape(R, 8, D // 8).transpose(1, 0, 2)

    def one_block(inputs):
        p_block, y_block, g_block = inputs
        new_block = p_block - jnp.dot(y_block.astype(jnp.float32), solved.astype(jnp.float32), precision=highest, preferred_element_type=jnp.float32)
        return (new_block, jnp.dot(g_block.astype(jnp.float32), new_block.astype(jnp.float32), precision=highest, preferred_element_type=jnp.float32))
    new_blocks, contribs = lax.map(one_block, (blocks, y_blocks, g_blocks))
    return (new_blocks.reshape(D, D), jnp.sum(contribs, axis=0))
```

```python
import functools

import jax
import jax.numpy as jnp
from jax import lax
from jax.experimental import pallas as pl
from jax.experimental.pallas import tpu as pltpu
from jax.sharding import PartitionSpec as P

HIGH = lax.Precision.HIGH
HIGHEST = lax.Precision.HIGHEST


def dot(a, b, precision):
    return jnp.dot(a, b, precision=precision, preferred_element_type=jnp.float32)


def dot_t(a, b, precision):
    return lax.dot_general(
        a, b, (((1,), (1,)), ((), ())),
        precision=precision, preferred_element_type=jnp.float32,
    )


def piece(x, index, size):
    return lax.dynamic_slice_in_dim(x, index * size, size, 0)


def from_ahead(x, axis, shift):
    n = lax.axis_size(axis)
    return lax.ppermute(x, axis, [(i, (i - shift) % n) for i in range(n)])


def swap_bit(x, axis, bit):
    n = lax.axis_size(axis)
    return lax.ppermute(x, axis, [(i, i ^ bit) for i in range(n)])


def gather_rows(x, beside):
    n, at, size = lax.axis_size("row"), lax.axis_index("row"), x.shape[0]
    blocks = [from_ahead(x, "row", shift) for shift in range(1, n)]
    blocks, beside = lax.optimization_barrier((blocks, beside))
    whole = jnp.zeros((size * n,) + x.shape[1:], x.dtype)
    for shift, block in enumerate([x] + blocks):
        whole = lax.dynamic_update_slice_in_dim(whole, block, (at + shift) % n * size, 0)
    return whole, beside


def scatter_rows(x):
    n, at = lax.axis_size("row"), lax.axis_index("row")
    size = x.shape[0] // n
    total = piece(x, at, size)
    for shift in range(1, n):
        total += from_ahead(piece(x, (at - shift) % n, size), "row", shift)
    return total


def all_reduce(x, axis):
    n = lax.axis_size(axis)
    if n & (n - 1) or x.shape[0] % n:
        return lax.psum(x, axis)
    done = []
    bit = 1
    while bit < n:
        half = x.shape[0] // 2
        side = lax.axis_index(axis) // bit % 2
        x = piece(x, side, half) + swap_bit(piece(x, 1 - side, half), axis, bit)
        done.append((bit, side))
        bit *= 2
    for bit, side in reversed(done):
        other = swap_bit(x, axis, bit)
        x = jnp.where(
            side == 0, jnp.concatenate([x, other]), jnp.concatenate([other, x])
        )
    return x


def invert_kernel(n, b, s_ref, o_ref):
    o_ref[...] = s_ref[...]
    lane = lax.broadcasted_iota(jnp.int32, (b, b), 1)
    sub = lax.broadcasted_iota(jnp.int32, (b, b), 0)

    def block(i, carry):
        span = pl.ds(pl.multiple_of(i * b, b), b)
        a = o_ref[span, span]
        for k in range(b):
            row, column = a[k : k + 1, :], a[:, k : k + 1]
            inverse = 1.0 / a[k : k + 1, k : k + 1]
            row = jnp.where(lane[:1] == k, 1.0, row) * inverse
            column = jnp.where(sub[:, :1] == k, -1.0, column)
            a = jnp.where((lane == k) | (sub == k), 0.0, a) - column * row
        side = o_ref[:, span]
        panel = dot(a, o_ref[span, :], HIGHEST)
        column = dot(side, a, HIGHEST)
        o_ref[...] -= dot(side, panel, HIGHEST)
        o_ref[span, :] = panel
        o_ref[:, span] = -column
        o_ref[span, span] = a
        return carry

    lax.fori_loop(0, n // b, block, 0)


def invert(system):
    n = system.shape[0]
    b = 128
    return pl.pallas_call(
        functools.partial(invert_kernel, n, b),
        out_shape=jax.ShapeDtypeStruct((n, n), jnp.float32),
        compiler_params=pltpu.CompilerParams(vmem_limit_bytes=16 << 20),
        cost_estimate=pl.CostEstimate(
            flops=40 * 10**9, bytes_accessed=8 * n * n, transcendentals=0
        ),
        name="invert",
    )(system)


def flip_kernel(x_ref, o_ref):
    o_ref[...] = x_ref[...].T


def flip(x):
    return pl.pallas_call(
        flip_kernel,
        out_shape=jax.ShapeDtypeStruct(x.shape[::-1], x.dtype),
        cost_estimate=pl.CostEstimate(
            flops=0, bytes_accessed=8 * x.size, transcendentals=0
        ),
        name="flip",
    )(x)


def split(x):
    top = x.astype(jnp.bfloat16)
    return top, (x - top.astype(jnp.float32)).astype(jnp.bfloat16)


def product(a, b):
    mul = functools.partial(jnp.dot, preferred_element_type=jnp.float32)
    return mul(a[1], b[0]) + mul(a[0], b[1]) + mul(a[0], b[0])


def times_kernel(part_ref, a_ref, p_ref, o_ref):
    a = a_ref[...].reshape(o_ref.shape[0], p_ref.shape[0])
    value = product(split(a), split(p_ref[...]))

    @pl.when(pl.program_id(0) == 0)
    def _():
        o_ref[...] = value

    @pl.when(pl.program_id(0) > 0)
    def _():
        o_ref[...] += value


def times(a, projector, name, part=0):
    height, width = projector.shape
    deep, tall = width, a.shape[-2]
    if a.ndim == 2:
        while deep % 128 and deep < height:
            deep *= 2
        spec = pl.BlockSpec((tall, deep), lambda j, at: (0, j))
    else:
        spec = pl.BlockSpec((1, 1, tall, width), lambda j, at: (at[0], j, 0, 0))
    return pl.pallas_call(
        times_kernel,
        grid_spec=pltpu.PrefetchScalarGridSpec(
            num_scalar_prefetch=1,
            grid=(height // deep,),
            in_specs=[spec, pl.BlockSpec((deep, width), lambda j, at: (j, 0))],
            out_specs=pl.BlockSpec((tall, width), lambda j, at: (0, 0)),
        ),
        out_shape=jax.ShapeDtypeStruct((tall, width), jnp.float32),
        compiler_params=pltpu.CompilerParams(vmem_limit_bytes=56 << 20),
        cost_estimate=pl.CostEstimate(
            flops=6 * tall * height * width,
            bytes_accessed=4 * height * (width + tall),
            transcendentals=0,
        ),
        name=name,
    )(jnp.full((1,), part, jnp.int32), a, projector)


def update_kernel(p_ref, y_ref, s_ref, o_ref, top_ref, low_ref):
    @pl.when(pl.program_id(0) == 0)
    def _():
        top_ref[...], low_ref[...] = split(s_ref[...])

    y = jnp.concatenate([y_ref[i, 0] for i in range(y_ref.shape[0])], axis=1)
    o_ref[...] = p_ref[...] - product(split(y), (top_ref[...], low_ref[...]))


def update(projector, y_parts, solved):
    height, width = projector.shape
    inner = solved.shape[0]
    parts, blocks, tall, part = y_parts.shape
    tile = tall
    return pl.pallas_call(
        update_kernel,
        grid=(height // tile,),
        in_specs=[
            pl.BlockSpec((tile, width), lambda m: (m, 0)),
            pl.BlockSpec((parts, 1, tile, part), lambda m: (0, m, 0, 0)),
            pl.BlockSpec((inner, width), lambda m: (0, 0)),
        ],
        out_specs=pl.BlockSpec((tile, width), lambda m: (m, 0)),
        out_shape=jax.ShapeDtypeStruct(projector.shape, jnp.float32),
        scratch_shapes=[pltpu.VMEM((inner, width), jnp.bfloat16)] * 2,
        compiler_params=pltpu.CompilerParams(vmem_limit_bytes=60 << 20),
        cost_estimate=pl.CostEstimate(
            flops=6 * height * width * inner,
            bytes_accessed=4 * height * (2 * width + inner),
            transcendentals=0,
        ),
        name="update",
    )(projector, y_parts, solved)


def local(projector, saved, grad_slab):
    rows, cols = lax.axis_size("row"), lax.axis_size("col")
    row = lax.axis_index("row")
    per_row = cols // rows
    cols_block = projector.shape[1]
    part = saved.shape[1]
    order = part * rows

    def to_home(x, beside=None):
        home = [
            (r * cols + c, (c // per_row) * cols + r * per_row + c % per_row)
            for r in range(rows)
            for c in range(cols)
        ]
        moved = lax.ppermute(x, ("row", "col"), [p for p in home if p[0] != p[1]])
        moved, beside = lax.optimization_barrier((moved, beside))
        here = row == lax.axis_index("col") // per_row
        return jnp.where(here, x, moved), beside

    tie = lax.optimization_barrier
    saved_t = flip(saved)
    saved_home, _ = to_home(saved_t)
    saved_rows = lax.all_gather(saved_home, "col", axis=0, tiled=True)
    saved_t, grad_slab, saved_rows = tie((saved_t, grad_slab, saved_rows))
    grad_rows = lax.all_gather(grad_slab, "col", axis=0, tiled=True)

    saved_rows = saved_rows.reshape(rows, per_row, part, cols_block)
    sent = []
    for shift in range(1, rows):
        other = times(saved_rows, projector, "y", (row - shift) % rows)
        if shift == 1:
            saved_cols, other = gather_rows(saved_t, other)
        sent.append(from_ahead(other, "row", shift))
    y_part = functools.reduce(jnp.add, sent, times(saved_rows, projector, "y", row))
    gram = all_reduce(dot_t(y_part, saved_cols, HIGHEST), "col")
    y_part, gram = tie((y_part, gram))

    first = times(grad_rows, projector, "g")
    gram, first = gather_rows(gram, first)
    y_home, first = to_home(flip(y_part), first)
    y_part, y_home, first, gram = tie((y_part, y_home, first, gram))
    y_rows = lax.all_gather(y_home, "col", axis=0, tiled=True)
    first = scatter_rows(first)
    inverse = invert(jnp.eye(order, dtype=jnp.float32) + gram)
    y_part, first, inverse = tie((y_part, first, inverse))
    grad_y = all_reduce(dot_t(first, saved_cols, HIGH), "col")
    y_cols, grad_y = gather_rows(y_part, grad_y)
    solved = dot(inverse, y_cols, HIGHEST)

    y_parts = y_rows.reshape(rows, per_row, cols_block, part)
    updated = update(projector, y_parts, solved)
    projected = first - dot(grad_y, solved, HIGH)
    return (updated, projected)


def solution(mesh):
    return jax.shard_map(
        local,
        mesh=mesh,
        in_specs=(P("row", "col"), P("col", "row"), P("col", "row")),
        out_specs=(P("row", "col"), P("row", "col")),
        check_vma=False,
    )
```

```python
import functools

import jax
import jax.numpy as jnp
from jax import lax
from jax.experimental import pallas as pl
from jax.experimental.pallas import tpu as pltpu
from jax.sharding import PartitionSpec as P

HIGH = lax.Precision.HIGH
HIGHEST = lax.Precision.HIGHEST


def dot(a, b, precision):
    return jnp.dot(a, b, precision=precision, preferred_element_type=jnp.float32)


def dot_t(a, b, precision):
    return lax.dot_general(
        a, b, (((1,), (1,)), ((), ())),
        precision=precision, preferred_element_type=jnp.float32,
    )


def piece(x, index, size):
    return lax.dynamic_slice_in_dim(x, index * size, size, 0)


def from_ahead(x, axis, shift):
    n = lax.axis_size(axis)
    return lax.ppermute(x, axis, [(i, (i - shift) % n) for i in range(n)])


def swap_bit(x, axis, bit):
    n = lax.axis_size(axis)
    return lax.ppermute(x, axis, [(i, i ^ bit) for i in range(n)])


def gather_rows(x, beside):
    n, at, size = lax.axis_size("row"), lax.axis_index("row"), x.shape[0]
    blocks = [from_ahead(x, "row", shift) for shift in range(1, n)]
    blocks, beside = lax.optimization_barrier((blocks, beside))
    whole = jnp.zeros((size * n,) + x.shape[1:], x.dtype)
    for shift, block in enumerate([x] + blocks):
        whole = lax.dynamic_update_slice_in_dim(whole, block, (at + shift) % n * size, 0)
    return whole, beside


def scatter_rows(x):
    n, at = lax.axis_size("row"), lax.axis_index("row")
    size = x.shape[0] // n
    total = piece(x, at, size)
    for shift in range(1, n):
        total += from_ahead(piece(x, (at - shift) % n, size), "row", shift)
    return total


def all_reduce(x, axis):
    n = lax.axis_size(axis)
    if n & (n - 1) or x.shape[0] % n:
        return lax.psum(x, axis)
    done = []
    bit = 1
    while bit < n:
        group = min(4, n // bit)
        size = x.shape[0] // group
        at = lax.axis_index(axis) // bit % group
        parts = [
            swap_bit(piece(x, at ^ step, size), axis, bit * step)
            for step in range(1, group)
        ]
        x = functools.reduce(jnp.add, parts, piece(x, at, size))
        done.append((bit, group, at))
        bit *= group
    for bit, group, at in reversed(done):
        size = x.shape[0]
        parts = [swap_bit(x, axis, bit * step) for step in range(1, group)]
        whole = jnp.zeros((size * group,) + x.shape[1:], x.dtype)
        for step, block in enumerate([x] + parts):
            whole = lax.dynamic_update_slice_in_dim(whole, block, (at ^ step) * size, 0)
        x = whole
    return x


def invert_kernel(n, b, s_ref, o_ref):
    o_ref[...] = s_ref[...]
    lane = lax.broadcasted_iota(jnp.int32, (b, b), 1)
    sub = lax.broadcasted_iota(jnp.int32, (b, b), 0)

    def block(i, carry):
        span = pl.ds(pl.multiple_of(i * b, b), b)
        a = o_ref[span, span]
        for k in range(b):
            row, column = a[k : k + 1, :], a[:, k : k + 1]
            inverse = 1.0 / a[k : k + 1, k : k + 1]
            row = jnp.where(lane[:1] == k, 1.0, row) * inverse
            column = jnp.where(sub[:, :1] == k, -1.0, column)
            a = jnp.where((lane == k) | (sub == k), 0.0, a) - column * row
        side = o_ref[:, span]
        panel = dot(a, o_ref[span, :], HIGHEST)
        column = dot(side, a, HIGHEST)
        o_ref[...] -= dot(side, panel, HIGHEST)
        o_ref[span, :] = panel
        o_ref[:, span] = -column
        o_ref[span, span] = a
        return carry

    lax.fori_loop(0, n // b, block, 0)


def invert(system):
    n = system.shape[0]
    b = 128
    return pl.pallas_call(
        functools.partial(invert_kernel, n, b),
        out_shape=jax.ShapeDtypeStruct((n, n), jnp.float32),
        compiler_params=pltpu.CompilerParams(vmem_limit_bytes=16 << 20),
        cost_estimate=pl.CostEstimate(
            flops=40 * 10**9, bytes_accessed=8 * n * n, transcendentals=0
        ),
        name="invert",
    )(system)


def flip_kernel(x_ref, o_ref):
    o_ref[...] = x_ref[...].T


def flip(x):
    return pl.pallas_call(
        flip_kernel,
        out_shape=jax.ShapeDtypeStruct(x.shape[::-1], x.dtype),
        cost_estimate=pl.CostEstimate(
            flops=0, bytes_accessed=8 * x.size, transcendentals=0
        ),
        name="flip",
    )(x)


def split(x):
    top = x.astype(jnp.bfloat16)
    return top, (x - top.astype(jnp.float32)).astype(jnp.bfloat16)


def product(a, b):
    mul = functools.partial(jnp.dot, preferred_element_type=jnp.float32)
    return mul(a[1], b[0]) + mul(a[0], b[1]) + mul(a[0], b[0])


def times_kernel(part_ref, a_ref, p_ref, o_ref):
    a = a_ref[...].reshape(o_ref.shape[0], p_ref.shape[0])
    value = product(split(a), split(p_ref[...]))

    @pl.when(pl.program_id(0) == 0)
    def _():
        o_ref[...] = value

    @pl.when(pl.program_id(0) > 0)
    def _():
        o_ref[...] += value


def times(a, projector, name, part=0):
    height, width = projector.shape
    deep, tall = width, a.shape[-2]
    if a.ndim == 2:
        while deep % 128 and deep < height:
            deep *= 2
        spec = pl.BlockSpec((tall, deep), lambda j, at: (0, j))
    else:
        spec = pl.BlockSpec((1, 1, tall, width), lambda j, at: (at[0], j, 0, 0))
    return pl.pallas_call(
        times_kernel,
        grid_spec=pltpu.PrefetchScalarGridSpec(
            num_scalar_prefetch=1,
            grid=(height // deep,),
            in_specs=[spec, pl.BlockSpec((deep, width), lambda j, at: (j, 0))],
            out_specs=pl.BlockSpec((tall, width), lambda j, at: (0, 0)),
        ),
        out_shape=jax.ShapeDtypeStruct((tall, width), jnp.float32),
        compiler_params=pltpu.CompilerParams(vmem_limit_bytes=56 << 20),
        cost_estimate=pl.CostEstimate(
            flops=6 * tall * height * width,
            bytes_accessed=4 * height * (width + tall),
            transcendentals=0,
        ),
        name=name,
    )(jnp.full((1,), part, jnp.int32), a, projector)


def update_kernel(p_ref, y_ref, s_ref, o_ref, top_ref, low_ref):
    @pl.when(pl.program_id(0) == 0)
    def _():
        top_ref[...], low_ref[...] = split(s_ref[...])

    y = jnp.concatenate([y_ref[i, 0] for i in range(y_ref.shape[0])], axis=1)
    o_ref[...] = p_ref[...] - product(split(y), (top_ref[...], low_ref[...]))


def update(projector, y_parts, solved):
    height, width = projector.shape
    inner = solved.shape[0]
    parts, blocks, tall, part = y_parts.shape
    tile = tall
    return pl.pallas_call(
        update_kernel,
        grid=(height // tile,),
        in_specs=[
            pl.BlockSpec((tile, width), lambda m: (m, 0)),
            pl.BlockSpec((parts, 1, tile, part), lambda m: (0, m, 0, 0)),
            pl.BlockSpec((inner, width), lambda m: (0, 0)),
        ],
        out_specs=pl.BlockSpec((tile, width), lambda m: (m, 0)),
        out_shape=jax.ShapeDtypeStruct(projector.shape, jnp.float32),
        scratch_shapes=[pltpu.VMEM((inner, width), jnp.bfloat16)] * 2,
        compiler_params=pltpu.CompilerParams(vmem_limit_bytes=60 << 20),
        cost_estimate=pl.CostEstimate(
            flops=6 * height * width * inner,
            bytes_accessed=4 * height * (2 * width + inner),
            transcendentals=0,
        ),
        name="update",
    )(projector, y_parts, solved)


def local(projector, saved, grad_slab):
    rows, cols = lax.axis_size("row"), lax.axis_size("col")
    row = lax.axis_index("row")
    per_row = cols // rows
    cols_block = projector.shape[1]
    part = saved.shape[1]
    order = part * rows

    def to_home(x, beside=None, cut=None):
        home = [
            (r * cols + c, (c // per_row) * cols + r * per_row + c % per_row)
            for r in range(rows)
            for c in range(cols)
        ]
        home = [p for p in home if p[0] != p[1]]
        both = ("row", "col")
        if cut and rows == 2:
            turn = [(i, j // cols * cols + i % cols) for i, j in home]
            along = [(j // cols * cols + i % cols, j) for i, j in home]
            tail = lax.ppermute(lax.ppermute(x[cut:], both, turn), both, along)
            moved = jnp.concatenate([lax.ppermute(x[:cut], both, home), tail])
        else:
            moved = lax.ppermute(x, both, home)
        moved, beside = lax.optimization_barrier((moved, beside))
        here = row == lax.axis_index("col") // per_row
        return jnp.where(here, x, moved), beside

    tie = lax.optimization_barrier
    saved_t = flip(saved)
    saved_home, _ = to_home(saved_t, cut=part * 5 // 64 * 8)
    saved_rows = lax.all_gather(saved_home, "col", axis=0, tiled=True)
    saved_t, grad_slab, saved_rows = tie((saved_t, grad_slab, saved_rows))
    grad_rows = lax.all_gather(grad_slab, "col", axis=0, tiled=True)

    saved_rows = saved_rows.reshape(rows, per_row, part, cols_block)
    sent = []
    for shift in range(1, rows):
        other = times(saved_rows, projector, "y", (row - shift) % rows)
        if shift == 1:
            saved_cols, other = gather_rows(saved_t, other)
        sent.append(from_ahead(other, "row", shift))
    y_part = functools.reduce(jnp.add, sent, times(saved_rows, projector, "y", row))
    gram = all_reduce(dot_t(y_part, saved_cols, HIGHEST), "col")
    y_part, gram = tie((y_part, gram))

    first = times(grad_rows, projector, "g")
    gram, first = gather_rows(gram, first)
    y_home, first = to_home(flip(y_part), first)
    y_part, y_home, first, gram = tie((y_part, y_home, first, gram))
    y_rows = lax.all_gather(y_home, "col", axis=0, tiled=True)
    first = scatter_rows(first)
    inverse = invert(jnp.eye(order, dtype=jnp.float32) + gram)
    y_part, first, inverse = tie((y_part, first, inverse))
    grad_y = all_reduce(dot_t(first, saved_cols, HIGH), "col")
    y_cols, grad_y = gather_rows(y_part, grad_y)
    solved = dot(inverse, y_cols, HIGHEST)

    y_parts = y_rows.reshape(rows, per_row, cols_block, part)
    updated = update(projector, y_parts, solved)
    projected = first - dot(grad_y, solved, HIGH)
    return (updated, projected)


def solution(mesh):
    return jax.shard_map(
        local,
        mesh=mesh,
        in_specs=(P("row", "col"), P("col", "row"), P("col", "row")),
        out_specs=(P("row", "col"), P("row", "col")),
        check_vma=False,
    )
```
